512 devices in a mesh: section: 16 (over x, y_hi, core), ctx: 32 (over z, y_lo).
Axes of the slice: x: 4, y: 4 (y_hi: 2, y_lo: 2; y = y_hi * 2 + y_lo), z: 16, core: 2. Of those that a mesh axis runs over, the one named last changes fastest.
Arguments:
- handoff: bfloat16 [16, 2, 3072, 4096], P('section', None, 'ctx'), may hold values from -500 to 500
- norm_gain: bfloat16 [16, 4096], P('section'), may hold values from 0.099609375 to 1.8984375
- kv_weight: bfloat16 [16, 4096, 1024], P('section', 'ctx'), may hold values from -0.09375 to 0.09375
- queries: bfloat16 [16, 2, 3072, 4096], P('section', None, 'ctx'), may hold values from -120 to 120
- span_order: int32 [2, 64], replicated, may hold values from 0 to 63, each once within a row
Outputs:
- partial_out: bfloat16 [16, 2, 3072, 4096], P('section', None, 'ctx')
- log_sum: float32 [16, 2, 32, 3072], P('section', None, None, 'ctx')
The draws below stay inside these ranges and needn't reach their ends.
Inputs may be any that keep to these rules, and one draw needn't show every extreme that they name: Each row of span_order names every span of 0 to 63 once.
All inputs are finite; a program needn't handle non-finite values.
Results may differ from the reference program's by a relative error of at most 0.012.
The reference program's roundings to bfloat16 on the way count: a program that leaves them out, or rounds other values in their place, can miss the bound.
Values may be sent and summed in bfloat16 or wider, within the bound.
A program may use at most 64 MiB of HBM per device.

```python
import math
import jax
import jax.numpy as jnp
from jax import lax

D = 4096
QH = 32
KVH = 4
HD = 128
TOK = 96
MB = 2
WINDOW = 4
SECTIONS = 16
SPAN = 48
SPANS = 64
SEQ = 3072
N_CTX = 32


def draw_handoff(key, part):
    base_key = jax.random.fold_in(key, 11)
    noise_key, row_key, col_key = jax.random.split(base_key, 3)
    row_scale = jnp.exp(jax.random.uniform(row_key, (SECTIONS, MB, SEQ, 1), jnp.float32, 0.0, math.log(10.0)))
    col_scale = jnp.exp(jax.random.uniform(col_key, (SECTIONS, 1, 1, D), jnp.float32, 0.0, math.log(10.0)))
    noise_vals = jnp.clip(jax.random.normal(noise_key, (SECTIONS, MB, SEQ, D), jnp.float32), -5.0, 5.0)
    return (noise_vals * row_scale * col_scale).astype(jnp.bfloat16)


def draw_queries(key, part):
    base_key = jax.random.fold_in(key, 23)
    noise_key = jax.random.fold_in(base_key, 0)
    values = 3.0 * jnp.clip(jax.random.normal(noise_key, (SECTIONS, MB, SEQ, QH, HD), jnp.float32), -5.0, 5.0)
    return values.reshape(SECTIONS, MB, SEQ, QH * HD).astype(jnp.bfloat16)


def levels(key, extent, cuts, least, high):
    gain, own = 1.0, jax.random.fold_in(key, 6)
    for position, shards_of in cuts:
        steps = jnp.exp(jax.random.uniform(jax.random.fold_in(own, position), (shards_of,), jnp.float32, least / len(cuts), high / len(cuts)))
        gain = gain * jnp.repeat(steps, extent[position] // shards_of).reshape([-1 if axis == position else 1 for axis in range(len(extent))])
    return gain


def centred(own_key, dims, width, bound, pieces=(), kind=jnp.bfloat16):
    loudness = levels(own_key, dims, pieces, -0.22, 0.18) if pieces else 1.0
    values = jax.random.normal(own_key, dims, jnp.float32) * width * loudness
    return jnp.minimum(jnp.maximum(values, -bound), bound).astype(kind)


def setup_inputs(seed: int = 0) -> dict:
    seeds = jax.random.split(jax.random.key(seed), 6)
    return {
        "handoff": draw_handoff(jax.random.fold_in(seeds[5], 71), 0),
        "norm_gain": jnp.clip(1.0 + 0.18 * jax.random.normal(seeds[1], (SECTIONS, D), jnp.float32), 0.099609375, 1.8984375).astype(jnp.bfloat16),
        "kv_weight": centred(seeds[2], (SECTIONS, D, 2 * KVH * HD), D ** -0.5, 0.09375, ((0, 16), (1, 32))),
        "queries": draw_queries(jax.random.fold_in(seeds[5], 71), 0),
        "span_order": jax.vmap(lambda own: jax.random.permutation(own, SPANS))(jax.random.split(seeds[4], MB)).reshape((MB, SPANS)).astype(jnp.int32),
    }


rope_base = 500000.0

def rotate(key_vecs, positions):
    half_dim = key_vecs.shape[-1] // 2
    frequency = rope_base ** (-2.0 * jnp.arange(half_dim, dtype=jnp.float32) / key_vecs.shape[-1])
    angles = positions.astype(jnp.float32)[..., None, None] * frequency
    cosine = jnp.cos(angles)
    sine_part = jnp.sin(angles)
    first_half = key_vecs[..., :half_dim]
    second = key_vecs[..., half_dim:]
    return jnp.concatenate([first_half * cosine - second * sine_part, second * cosine + first_half * sine_part], axis=-1)

def reference(handoff, norm_gain, kv_weight, queries, span_order):
    layer_in = jnp.roll(handoff, 1, axis=0)
    offsets = (jnp.arange(SEQ) % SPAN).astype(jnp.int32)
    slots = (jnp.arange(SEQ) // SPAN).astype(jnp.int32)
    positions = (span_order[:, slots] * SPAN + offsets[None, :]).astype(jnp.int32)
    key_pos = positions.reshape(MB, N_CTX, TOK)
    window_pos = jnp.concatenate([jnp.roll(key_pos, step_num, axis=1) for step_num in range(WINDOW)], axis=2)
    group_size = QH // KVH

    def one_section(inputs):
        section_in, section_gain, weight, query_block = inputs
        activations = section_in.astype(jnp.float32)
        scale = lax.rsqrt(lax.optimization_barrier(jnp.mean(activations * activations, axis=-1, keepdims=True)) + 1e-05)
        normed = (activations * scale * section_gain.astype(jnp.float32)).astype(jnp.bfloat16)
        kv_rows = jnp.dot(normed.reshape(MB * SEQ, D), weight, preferred_element_type=jnp.float32)
        kv_rows = kv_rows.reshape(MB, SEQ, 2, KVH, HD)
        key_block = rotate(kv_rows[:, :, 0], positions).astype(jnp.bfloat16).reshape(MB, N_CTX, TOK, KVH, HD)
        value_block = kv_rows[:, :, 1].astype(jnp.bfloat16).reshape(MB, N_CTX, TOK, KVH, HD)
        window_keys = jnp.concatenate([jnp.roll(key_block, step_num, axis=1) for step_num in range(WINDOW)], axis=2)
        window_values = jnp.concatenate([jnp.roll(value_block, step_num, axis=1) for step_num in range(WINDOW)], axis=2)
        query_rows = query_block.reshape(MB, N_CTX, TOK, KVH, group_size, HD).astype(jnp.float32)
        scores = jnp.einsum('mctkgd,mcukd->mckgtu', query_rows, window_keys.astype(jnp.float32)) * HD ** (-0.5)
        visible = window_pos[:, :, None, None, None, :] <= key_pos[:, :, None, None, :, None]
        scores = jnp.where(visible, scores, -jnp.inf)
        row_max = lax.optimization_barrier(jnp.max(scores, axis=-1, keepdims=True))
        exps = jnp.exp(scores - row_max)
        running = lax.optimization_barrier(jnp.sum(exps, axis=-1, keepdims=True))
        log_sums = (row_max + jnp.log(running))[..., 0]
        weights_bf = lax.optimization_barrier(exps.astype(jnp.bfloat16))
        mixed = jnp.einsum('mckgtu,mcukd->mctkgd', weights_bf.astype(jnp.float32), window_values.astype(jnp.float32))
        denominator = jnp.moveaxis(running[..., 0], 4, 2)[..., None]
        result = (mixed / denominator).astype(jnp.bfloat16).reshape(MB, SEQ, QH * HD)
        log_result = jnp.transpose(log_sums, (0, 2, 3, 1, 4)).reshape(MB, QH, SEQ)
        return (result, log_result)
    partial_out, log_sum = lax.map(one_section, (layer_in, norm_gain, kv_weight, queries))
    return (partial_out, log_sum)
```

```python
import functools
import math

import jax
import jax.numpy as jnp
import numpy as np
from jax import lax
from jax.experimental import pallas as pl
from jax.experimental.pallas import tpu as pltpu
from jax.sharding import PartitionSpec as P

QH = 32
KVH = 4
HD = 128
GROUP = QH // KVH
SPAN = 48
TOK = 96
MB = 2
D = 4096
ROWS = MB * TOK
WIN = 5 * TOK
SEEN = 4 * TOK
MESH = pl.DeviceIdType.MESH
PARTS = 4
PART = ROWS // PARTS
LAG = 8
LOG2E = math.log2(math.e)
LN2 = math.log(2.0)
rope_base = 500000.0


def kernel(
    sections, ring,
    order, freq, gain, hand, weight, queries,
    out, lse,
    x_buf, xn, w_buf, acc, win, q_buf, o_buf, probs, recip, cosine, sine, bias, lbuf,
    loc_sem, w_recv, w_up, w_dn, w_mate, x_recv, x_send, win_recv, win_send, out_sem,
):
    s = lax.axis_index("section")
    c = lax.axis_index("ctx")
    z = c // 2
    y = lax.rem(c, 2)
    other = 1 - y
    mate = 2 * z + other
    half = ring // 2
    even = lax.rem(s, 2) == 0
    nxt = lax.rem(s + 1, sections)
    prv = lax.rem(s + sections - 1, sections)

    def at_z(step):
        return lax.rem(z + step + ring, ring)

    up = {"ctx": 2 * at_z(1) + y}
    dn = {"ctx": 2 * at_z(-1) + y}
    far = {"ctx": 2 * at_z(2)}
    back = at_z(-2)
    mate_id = {"ctx": mate}

    barrier = pltpu.get_barrier_semaphore()

    def greet(device):
        pl.semaphore_signal(barrier, inc=1, device_id=device, device_id_type=MESH)

    for device in (
        up, dn, mate_id,
        {"section": nxt, "ctx": c}, {"section": prv, "ctx": c},
        {"section": nxt, "ctx": mate}, {"section": prv, "ctx": mate},
        far,
    ):
        greet(device)

    @pl.when(y == 0)
    def _():
        greet({"ctx": 2 * back})
        greet({"ctx": 2 * back + 1})
        pl.semaphore_wait(barrier, 10)

    @pl.when(y == 1)
    def _():
        pl.semaphore_wait(barrier, 8)

    def remote(src, dst, send, recv, device):
        return pltpu.make_async_remote_copy(
            src_ref=src, dst_ref=dst, send_sem=send, recv_sem=recv,
            device_id=device, device_id_type=MESH,
        )

    def w_cols(p, h):
        return weight.at[:, pl.ds(pl.multiple_of(p * 512 + h * 256, 256), 256)]

    def w_slot(p, chunk, b):
        return w_buf.at[p, chunk, pl.ds(pl.multiple_of(b * 128, 128), 128)]

    def w_local(p):
        return pltpu.make_async_copy(w_cols(p, y), w_slot(p, z, y), loc_sem.at[p])

    def w_cross(p, b):
        return remote(w_cols(p, other), w_slot(p, z, b), w_mate.at[p], w_recv.at[p, z, b], mate_id)

    for p in range(2):
        w_local(p).start()
        w_cross(p, y).start()

    def x_rows(b, r):
        return x_buf.at[b, pl.ds(r * PART, PART)]

    def x_copy(kind, src, b, r, device):
        return remote(src, x_rows(b, r), x_send.at[kind, r], x_recv.at[b, r], device)

    def x_cross(r):
        return x_copy(0, hand.at[pl.ds(r * PART, PART)], y, r, {"section": nxt, "ctx": mate})

    def x_direct(r):
        return x_copy(1, hand.at[pl.ds(r * PART, PART)], y, r, {"section": nxt, "ctx": c})

    def x_onward(r):
        return x_copy(2, x_rows(other, r), other, r, mate_id)

    def x_arrived(b, r):
        x_copy(0, x_rows(b, r), b, r, mate_id).wait_recv()

    for r in range(PARTS):
        x_cross(r).start()

        @pl.when(even)
        def _():
            x_direct(r).start()

    q_copy = pltpu.make_async_copy(queries, q_buf, loc_sem.at[2])
    q_copy.start()

    def w_hop(p, k, b, upward):
        chunk = at_z(-k if upward else k)
        sems = w_up if upward else w_dn
        slot = w_slot(p, chunk, b)
        return remote(slot, slot, sems.at[p, k, b], w_recv.at[p, chunk, b], up if upward else dn)

    def ring_step(p, k):
        for b in (y, other):
            if k == 0:
                if b is y:
                    w_local(p).wait()
                else:
                    w_cross(p, other).wait_recv()
            else:
                if k < half:
                    w_hop(p, k, b, True).wait_recv()
                w_hop(p, k, b, False).wait_recv()
            if k < half - 1:
                w_hop(p, k, b, True).start()
            if k < half:
                w_hop(p, k, b, False).start()

    def slots(p, h, first, count):
        return win.at[p, pl.ds(2 * h, 2), :, pl.ds(first * TOK, count * TOK)]

    def to_up(p):
        return remote(slots(p, y, 3, 2), slots(p, y, 1, 2), win_send.at[p, 0], win_recv.at[p, 0], up)

    def to_far(p, h):
        return remote(slots(p, y, 4, 1), slots(p, h, 0, 1), win_send.at[p, 1], win_recv.at[p, 1 + h], far)

    def to_mate(p, h):
        return remote(slots(p, h, 3, 1), slots(p, h, 3, 1), win_send.at[p, 2], win_recv.at[p, 3], mate_id)

    def to_mate_last(p, h):
        return remote(slots(p, h, 4, 1), slots(p, h, 4, 1), win_send.at[p, 3], win_recv.at[p, 4], mate_id)

    def to_mate_old(p, h):
        return remote(slots(p, h, 1, 2), slots(p, h, 1, 2), win_send.at[p, 4], win_recv.at[p, 5], mate_id)

    def window_out(p):
        to_up(p).start()
        to_mate(p, y).start()

        @pl.when(y == 0)
        def _():
            to_mate_last(p, y).start()

        to_far(p, y).start()

    def window_onward(p):
        to_up(p).wait_recv()
        to_mate_old(p, y).start()

    def window_arrived(p):
        to_mate(p, other).wait_recv()
        to_mate_old(p, other).wait_recv()

        @pl.when(y == 0)
        def _():
            to_far(p, 0).wait_recv()
            to_far(p, 1).wait_recv()

        @pl.when(y == 1)
        def _():
            to_mate_last(p, other).wait_recv()

    def tables():
        row = lax.broadcasted_iota(jnp.int32, (SPAN, HD), 0)
        low = lax.broadcasted_iota(jnp.int32, (SPAN, HD), 1) < HD // 2
        for b in range(2):
            for m in range(MB):
                for i in range(2):
                    span = order[m, 4 * z + 2 * b + i]
                    angle = (span * SPAN + row).astype(jnp.float32) * freq[...]
                    first = b * ROWS + m * TOK + i * SPAN
                    cosine[pl.ds(first, SPAN), :] = jnp.cos(angle)
                    turned = jnp.sin(angle)
                    sine[pl.ds(first, SPAN), :] = jnp.where(low, -turned, turned)

    def masks():
        lane = lax.broadcasted_iota(jnp.int32, (SPAN, SEEN), 1)
        row = lax.broadcasted_iota(jnp.int32, (SPAN, SEEN), 0)
        for m in range(MB):
            key_pos = lane
            for j in range(4):
                block = lax.rem(c - 3 + j + 2 * ring, 2 * ring)
                for i in range(2):
                    n = 2 * j + i
                    here = lane >= n * SPAN
                    key_pos = jnp.where(here, order[m, 2 * block + i] * SPAN + lane - n * SPAN, key_pos)
            for i in range(2):
                own_pos = order[m, 2 * c + i] * SPAN + row
                bias[m, pl.ds(i * SPAN, SPAN), :] = jnp.where(key_pos <= own_pos, 0.0, -jnp.inf)

    def normalise(b, r):
        first = pl.multiple_of(b * ROWS + r * PART, 16)
        values = x_buf[b, pl.ds(r * PART, PART), :].astype(jnp.float32)
        scale = lax.rsqrt(jnp.mean(values * values, axis=-1, keepdims=True) + 1e-05)
        scaled = values * scale * gain[...].astype(jnp.float32)
        xn[pl.ds(first, PART), :] = scaled.astype(jnp.bfloat16)

    def product(p, chunk):
        columns = pl.ds(pl.multiple_of(chunk * 256, 256), 256)
        return jnp.dot(xn[:, columns], w_buf[p, chunk], preferred_element_type=jnp.float32)

    def keys():
        acc[...] = jnp.zeros_like(acc)

        def add(chunk, _):
            acc[...] += product(0, chunk)
            return 0

        lax.fori_loop(0, ring, add, 0)
        for sub in range(2):
            part = acc[:, sub * HD : (sub + 1) * HD]
            turned = part * cosine[...] + pltpu.roll(part, HD // 2, 1) * sine[...]
            store(0, sub, turned)
        acc[...] = jnp.zeros_like(acc)

    def store(p, sub, rows):
        rows = rows.astype(jnp.bfloat16)
        for b in range(2):
            for m in range(MB):
                win[p, 2 * y + sub, m, pl.ds((3 + b) * TOK, TOK), :] = rows[
                    b * ROWS + m * TOK : b * ROWS + (m + 1) * TOK
                ]

    def value_step(k):
        if k < half:
            acc[...] += product(1, at_z(-k))
        if k > 0:
            acc[...] += product(1, at_z(k))

    def score(n, _):
        m = lax.rem(n, MB)
        head = lax.rem(2 * y + n // MB, KVH)
        q = jnp.concatenate(
            [
                q_buf[pl.ds(pl.multiple_of(m * TOK, TOK), TOK), pl.ds(pl.multiple_of((head * GROUP + g) * HD, HD), HD)]
                for g in range(GROUP)
            ],
            axis=0,
        )
        k = win[0, head, m, pl.ds(pl.multiple_of(y * TOK, TOK), SEEN), :]
        raw = lax.dot_general(q, k, (((1,), (1,)), ((), ())), preferred_element_type=jnp.float32)
        raw = raw.reshape(GROUP, TOK, SEEN) * (HD ** -0.5 * LOG2E) + bias[m][None]
        top = jnp.max(raw, axis=-1, keepdims=True)
        exps = jnp.exp2(raw - top)
        total = jnp.sum(exps, axis=-1, keepdims=True)
        probs[n] = exps.astype(jnp.bfloat16).reshape(GROUP * TOK, SEEN)
        recip[n] = jnp.broadcast_to(1.0 / total, (GROUP, TOK, HD))
        logs = top * LN2 + jnp.log(total)
        lane = lax.broadcasted_iota(jnp.int32, (TOK, HD), 1)
        kept = lbuf[m]
        for g in range(GROUP):
            kept = jnp.where(lane == head * GROUP + g, logs[g], kept)
        lbuf[m] = kept
        return 0

    def out_copy(n):
        m = lax.rem(n, MB)
        head = lax.rem(2 * y + n // MB, KVH)
        view = (
            pl.ds(pl.multiple_of(m * TOK, TOK), TOK),
            pl.ds(pl.multiple_of(head * GROUP * HD, GROUP * HD), GROUP * HD),
        )
        return pltpu.make_async_copy(o_buf.at[view], out.at[view], out_sem.at[n])

    def mix(n, _):
        m = lax.rem(n, MB)
        head = lax.rem(2 * y + n // MB, KVH)
        v = win[1, head, m, pl.ds(pl.multiple_of(y * TOK, TOK), SEEN), :]
        mixed = jnp.dot(probs[n], v, preferred_element_type=jnp.float32)
        mixed = (mixed.reshape(GROUP, TOK, HD) * recip[n]).astype(jnp.bfloat16)
        for g in range(GROUP):
            o_buf[
                pl.ds(pl.multiple_of(m * TOK, TOK), TOK),
                pl.ds(pl.multiple_of((head * GROUP + g) * HD, HD), HD),
            ] = mixed[g]
        out_copy(n).start()
        return 0

    def onward(r):
        @pl.when(even)
        def _():
            x_arrived(other, r)
            x_onward(r).start()

    def ready(b, r):
        if b is other:
            @pl.when(jnp.logical_not(even))
            def _():
                x_arrived(other, r)
        else:
            x_arrived(y, r)

    for t in range(LAG + half + 1):
        if t <= half:
            ring_step(0, t)
        if 0 <= t - LAG <= half:
            ring_step(1, t - LAG)
        if t == 0:
            tables()
        if t == 1:
            masks()
            lbuf[...] = jnp.zeros_like(lbuf)
        if t in (3, 5, 7, 8):
            onward((3, 5, 7, 8).index(t))
        if t in (9, 10):
            for r in (2 * (t - 9), 2 * (t - 9) + 1):
                ready(other, r)
                normalise(other, r)
        if t in (11, 12):
            for r in (2 * (t - 11), 2 * (t - 11) + 1):
                ready(y, r)
                normalise(y, r)
        if t == 12:
            keys()
            window_out(0)
            for k in range(t - LAG + 1):
                value_step(k)
        if t > 12:
            value_step(t - LAG)
        if t == 15:
            window_onward(0)

    for sub in range(2):
        store(1, sub, acc[:, sub * HD : (sub + 1) * HD])
    window_out(1)
    q_copy.wait()
    window_arrived(0)
    lax.fori_loop(0, KVH, score, 0)
    window_onward(1)
    lax.fori_loop(KVH, MB * KVH, score, 0)
    for m in range(MB):
        lse[m] = lbuf[m].T[:QH, :]
    window_arrived(1)
    lax.fori_loop(0, MB * KVH, mix, 0)

    for p in range(2):
        w_cross(p, y).wait_send()
        for k in range(half):
            for b in range(2):
                if k < half - 1:
                    w_hop(p, k, b, True).wait_send()
                w_hop(p, k, b, False).wait_send()
        to_up(p).wait_send()
        to_far(p, y).wait_send()
        to_mate(p, y).wait_send()
        to_mate_old(p, y).wait_send()

        @pl.when(y == 0)
        def _():
            to_mate_last(p, y).wait_send()

    for r in range(PARTS):
        x_cross(r).wait_send()

        @pl.when(even)
        def _():
            x_direct(r).wait_send()
            x_onward(r).wait_send()

    for n in range(MB * KVH):
        out_copy(n).wait()


def solution(mesh):
    sections, n_ctx = mesh.shape["section"], mesh.shape["ctx"]
    ring = n_ctx // 2
    half = ring // 2

    def on_device(handoff, norm_gain, kv_weight, queries, span_order):
        freq = rope_base ** (-2.0 * np.arange(HD // 2, dtype=np.float64) / HD)
        freq = jnp.asarray(np.concatenate([freq, freq])[None].astype(np.float32))
        any_space = pl.BlockSpec(memory_space=pl.ANY)
        vmem = pl.BlockSpec(memory_space=pltpu.VMEM)
        dma = pltpu.SemaphoreType.DMA
        bf16, f32 = jnp.bfloat16, jnp.float32
        out, lse = pl.pallas_call(
            functools.partial(kernel, sections, ring),
            out_shape=(
                jax.ShapeDtypeStruct((ROWS, D), bf16),
                jax.ShapeDtypeStruct((MB, QH, TOK), f32),
            ),
            in_specs=[pl.BlockSpec(memory_space=pltpu.SMEM), vmem, vmem, any_space, any_space, any_space],
            out_specs=(any_space, vmem),
            scratch_shapes=[
                pltpu.VMEM((2, ROWS, D), bf16),
                pltpu.VMEM((2 * ROWS, D), bf16),
                pltpu.VMEM((2, ring, 256, 256), bf16),
                pltpu.VMEM((2 * ROWS, 256), f32),
                pltpu.VMEM((2, KVH, MB, WIN, HD), bf16),
                pltpu.VMEM((ROWS, D), bf16),
                pltpu.VMEM((ROWS, D), bf16),
                pltpu.VMEM((MB * KVH, GROUP * TOK, SEEN), bf16),
                pltpu.VMEM((MB * KVH, GROUP, TOK, HD), f32),
                pltpu.VMEM((2 * ROWS, HD), f32),
                pltpu.VMEM((2 * ROWS, HD), f32),
                pltpu.VMEM((MB, TOK, SEEN), f32),
                pltpu.VMEM((MB, TOK, HD), f32),
                dma((3,)),
                dma((2, ring, 2)),
                dma((2, half, 2)),
                dma((2, half, 2)),
                dma((2,)),
                dma((2, PARTS)),
                dma((3, PARTS)),
                dma((2, 6)),
                dma((2, 5)),
                dma((MB * KVH,)),
            ],
            compiler_params=pltpu.CompilerParams(
                collective_id=0, has_side_effects=True, vmem_limit_bytes=56 << 20
            ),
            name="relay",
        )(
            span_order, freq, norm_gain, handoff.reshape(ROWS, D), kv_weight[0], queries.reshape(ROWS, D),
        )
        return out.reshape(1, MB, TOK, D), lse[None]

    placed = (
        P("section", None, "ctx", None),
        P("section", None),
        P("section", "ctx", None),
        P("section", None, "ctx", None),
        P(),
    )
    return jax.shard_map(
        on_device,
        mesh=mesh,
        in_specs=placed,
        out_specs=(P("section", None, "ctx", None), P("section", None, None, "ctx")),
        check_vma=False,
    )
```

```python
import functools
import math

import jax
import jax.numpy as jnp
import numpy as np
from jax import lax
from jax.experimental import pallas as pl
from jax.experimental.pallas import tpu as pltpu
from jax.sharding import PartitionSpec as P

QH = 32
KVH = 4
HD = 128
GROUP = QH // KVH
SPAN = 48
TOK = 96
MB = 2
D = 4096
ROWS = MB * TOK
WIN = 5 * TOK
SEEN = 4 * TOK
MESH = pl.DeviceIdType.MESH
PARTS = 4
PART = ROWS // PARTS
LAG = 1
SUBS = 2
ONWARD = (1, 2, 3, 4)
NORMED = 7
LOG2E = math.log2(math.e)
LN2 = math.log(2.0)
rope_base = 500000.0


def kernel(
    sections, ring,
    order_in, freq_in, gain_in, hand, weight, queries,
    out, lse,
    order, freq, gain, x_buf, xn, w_buf, acc, win, q_buf, probs, recip, cosine, sine, bias, lbuf,
    loc_sem, w_recv, w_up, w_dn, w_mate, x_recv, x_send, win_recv, win_send,
):
    s = lax.axis_index("section")
    c = lax.axis_index("ctx")
    z = c // 2
    y = lax.rem(c, 2)
    other = 1 - y
    mate = 2 * z + other
    half = ring // 2
    even = lax.rem(s, 2) == 0
    nxt = lax.rem(s + 1, sections)
    prv = lax.rem(s + sections - 1, sections)

    def at_z(step):
        return lax.rem(z + step + ring, ring)

    up = {"ctx": 2 * at_z(1) + y}
    dn = {"ctx": 2 * at_z(-1) + y}
    far = {"ctx": 2 * at_z(2)}
    back = at_z(-2)
    mate_id = {"ctx": mate}

    barrier = pltpu.get_barrier_semaphore()

    def greet(device):
        pl.semaphore_signal(barrier, inc=1, device_id=device, device_id_type=MESH)

    for device in (
        up, dn, mate_id,
        {"section": nxt, "ctx": c}, {"section": prv, "ctx": c},
        {"section": nxt, "ctx": mate}, {"section": prv, "ctx": mate},
        far,
    ):
        greet(device)

    @pl.when(y == 0)
    def _():
        greet({"ctx": 2 * back})
        greet({"ctx": 2 * back + 1})

    def remote(src, dst, send, recv, device):
        return pltpu.make_async_remote_copy(
            src_ref=src, dst_ref=dst, send_sem=send, recv_sem=recv,
            device_id=device, device_id_type=MESH,
        )

    def w_cols(p, h):
        return weight.at[:, pl.ds(pl.multiple_of(p * 512 + h * 256, 256), 256)]

    def w_slot(p, chunk, b):
        return w_buf.at[p, chunk, pl.ds(pl.multiple_of(b * 128, 128), 128)]

    def w_local(p):
        return pltpu.make_async_copy(w_cols(p, y), w_slot(p, z, y), loc_sem.at[p])

    def w_cross(p, b):
        return remote(w_cols(p, other), w_slot(p, z, b), w_mate.at[p], w_recv.at[p, z, b, 0], mate_id)

    fetches = [
        pltpu.make_async_copy(src, dst, loc_sem.at[2 + i])
        for i, (src, dst) in enumerate(
            ((order_in, order), (freq_in, freq), (gain_in, gain), (queries, q_buf))
        )
    ]
    for p in range(2):
        w_local(p).start()
    for fetch in fetches:
        fetch.start()

    @pl.when(y == 0)
    def _():
        pl.semaphore_wait(barrier, 10)

    @pl.when(y == 1)
    def _():
        pl.semaphore_wait(barrier, 8)

    for p in range(2):
        w_cross(p, y).start()

    def x_rows(b, r):
        return x_buf.at[b, pl.ds(r * PART, PART)]

    def x_copy(kind, src, b, r, device):
        return remote(src, x_rows(b, r), x_send.at[kind, r], x_recv.at[b, r], device)

    def x_cross(r):
        return x_copy(0, hand.at[pl.ds(r * PART, PART)], y, r, {"section": nxt, "ctx": mate})

    def x_direct(r):
        return x_copy(1, hand.at[pl.ds(r * PART, PART)], y, r, {"section": nxt, "ctx": c})

    def x_onward(r):
        return x_copy(2, x_rows(other, r), other, r, mate_id)

    def x_arrived(b, r):
        x_copy(0, x_rows(b, r), b, r, mate_id).wait_recv()

    def w_hop(p, k, b, u, upward):
        chunk = at_z(-k if upward else k)
        sems = w_up if upward else w_dn
        rows = 128 // SUBS
        slot = w_buf.at[p, chunk, pl.ds(pl.multiple_of(b * 128 + u * rows, rows), rows)]
        src = slot
        if k == 0 and b is y:
            src = weight.at[
                pl.ds(u * rows, rows), pl.ds(pl.multiple_of(p * 512 + y * 256, 256), 256)
            ]
        return remote(
            src, slot, sems.at[p, k, b, u], w_recv.at[p, chunk, b, u], up if upward else dn
        )

    def hops(k, u, upward):
        if k < half - 1:
            return True
        return k == half - 1 and (u < SUBS // 2) == upward

    def ring_step(p, k):
        for b in (y, other):
            if k == 0 and b is other:
                w_cross(p, other).wait_recv()
            for u in range(SUBS):
                for upward in (True, False):
                    if k > 0 and hops(k - 1, u, upward):
                        w_hop(p, k, b, u, upward).wait_recv()
                    if hops(k, u, upward):
                        w_hop(p, k, b, u, upward).start()

    def slots(p, heads, first, count):
        return win.at[p, heads, :, pl.ds(first * TOK, count * TOK)]

    def pair(h):
        return pl.ds(2 * h, 2)

    def to_up(p, sub):
        head = 2 * y + sub
        return remote(
            slots(p, head, 3, 2), slots(p, head, 1, 2), win_send.at[p, sub], win_recv.at[p, sub], up
        )

    def to_far(p, h):
        return remote(
            slots(p, pair(y), 4, 1), slots(p, pair(h), 0, 1), win_send.at[p, 2], win_recv.at[p, 2 + h], far
        )

    def to_mate(p, h):
        both = slots(p, pair(h), 3, 1)
        return remote(both, both, win_send.at[p, 3], win_recv.at[p, 4], mate_id)

    def to_mate_last(p, h):
        both = slots(p, pair(h), 4, 1)
        return remote(both, both, win_send.at[p, 4], win_recv.at[p, 5], mate_id)

    def to_mate_old(p, h, sub):
        old = slots(p, 2 * h + sub, 1, 2)
        return remote(old, old, win_send.at[p, 5 + sub], win_recv.at[p, 6 + sub], mate_id)

    def window_out(p):
        for sub in range(2):
            to_up(p, sub).start()
        to_mate(p, y).start()

        @pl.when(y == 0)
        def _():
            to_mate_last(p, y).start()

        to_far(p, y).start()

    def window_onward(p, sub):
        to_up(p, sub).wait_recv()
        to_mate_old(p, y, sub).start()

    def own_arrived(p):
        @pl.when(y == 0)
        def _():
            to_far(p, 0).wait_recv()

    def others_arrived(p):
        to_mate(p, other).wait_recv()
        for sub in range(2):
            to_mate_old(p, other, sub).wait_recv()

        @pl.when(y == 0)
        def _():
            to_far(p, 1).wait_recv()

        @pl.when(y == 1)
        def _():
            to_mate_last(p, other).wait_recv()

    def tables():
        row = lax.broadcasted_iota(jnp.int32, (SPAN, HD), 0)
        low = lax.broadcasted_iota(jnp.int32, (SPAN, HD), 1) < HD // 2
        for b in range(2):
            for m in range(MB):
                for i in range(2):
                    span = order[m, 4 * z + 2 * b + i]
                    angle = (span * SPAN + row).astype(jnp.float32) * freq[...]
                    first = b * ROWS + m * TOK + i * SPAN
                    cosine[pl.ds(first, SPAN), :] = jnp.cos(angle)
                    turned = jnp.sin(angle)
                    sine[pl.ds(first, SPAN), :] = jnp.where(low, -turned, turned)

    def masks():
        lane = lax.broadcasted_iota(jnp.int32, (SPAN, SEEN), 1)
        row = lax.broadcasted_iota(jnp.int32, (SPAN, SEEN), 0)
        for m in range(MB):
            key_pos = lane
            for j in range(4):
                block = lax.rem(c - 3 + j + 2 * ring, 2 * ring)
                for i in range(2):
                    n = 2 * j + i
                    here = lane >= n * SPAN
                    key_pos = jnp.where(here, order[m, 2 * block + i] * SPAN + lane - n * SPAN, key_pos)
            for i in range(2):
                own_pos = order[m, 2 * c + i] * SPAN + row
                bias[m, pl.ds(i * SPAN, SPAN), :] = jnp.where(key_pos <= own_pos, 0.0, -jnp.inf)

    def normalise(b, r):
        first = pl.multiple_of(b * ROWS + r * PART, 16)
        values = x_buf[b, pl.ds(r * PART, PART), :].astype(jnp.float32)
        scale = lax.rsqrt(jnp.mean(values * values, axis=-1, keepdims=True) + 1e-05)
        scaled = values * scale * gain[...].astype(jnp.float32)
        xn[pl.ds(first, PART), :] = scaled.astype(jnp.bfloat16)

    def product(p, chunk):
        columns = pl.ds(pl.multiple_of(chunk * 256, 256), 256)
        return jnp.dot(xn[:, columns], w_buf[p, chunk], preferred_element_type=jnp.float32)

    def keys():
        for sub in range(2):
            part = acc[0, :, sub * HD : (sub + 1) * HD]
            turned = part * cosine[...] + pltpu.roll(part, HD // 2, 1) * sine[...]
            store(0, sub, turned)

    def values():
        for sub in range(2):
            store(1, sub, acc[1, :, sub * HD : (sub + 1) * HD])

    def store(p, sub, rows):
        rows = rows.astype(jnp.bfloat16)
        for b in range(2):
            for m in range(MB):
                win[p, 2 * y + sub, m, pl.ds((3 + b) * TOK, TOK), :] = rows[
                    b * ROWS + m * TOK : b * ROWS + (m + 1) * TOK
                ]

    def add(p, k):
        if k == 0:
            w_local(p).wait()
        total = product(p, at_z(k))
        if 0 < k < half:
            total += product(p, at_z(-k))
        if k == 0:
            acc[p] = total
        else:
            acc[p] += total

    def score(n, _):
        m = lax.rem(n, MB)
        head = lax.rem(2 * y + n // MB, KVH)
        q = jnp.concatenate(
            [
                q_buf[pl.ds(pl.multiple_of(m * TOK, TOK), TOK), pl.ds(pl.multiple_of((head * GROUP + g) * HD, HD), HD)]
                for g in range(GROUP)
            ],
            axis=0,
        )
        k = win[0, head, m, pl.ds(pl.multiple_of(y * TOK, TOK), SEEN), :]
        raw = lax.dot_general(q, k, (((1,), (1,)), ((), ())), preferred_element_type=jnp.float32)
        raw = raw.reshape(GROUP, TOK, SEEN) * (HD ** -0.5 * LOG2E) + bias[m][None]
        top = jnp.max(raw, axis=-1, keepdims=True)
        exps = jnp.exp2(raw - top)
        total = jnp.sum(exps, axis=-1, keepdims=True)
        probs[n] = exps.astype(jnp.bfloat16).reshape(GROUP * TOK, SEEN)
        recip[n] = jnp.broadcast_to(1.0 / total, (GROUP, TOK, HD))
        logs = top * LN2 + jnp.log(total)
        lane = lax.broadcasted_iota(jnp.int32, (TOK, HD), 1)
        kept = lbuf[m]
        for g in range(GROUP):
            kept = jnp.where(lane == head * GROUP + g, logs[g], kept)
        lbuf[m] = kept
        return 0

    def mix(n, _):
        m = lax.rem(n, MB)
        head = lax.rem(2 * y + n // MB, KVH)
        v = win[1, head, m, pl.ds(pl.multiple_of(y * TOK, TOK), SEEN), :]
        mixed = jnp.dot(probs[n], v, preferred_element_type=jnp.float32)
        mixed = (mixed.reshape(GROUP, TOK, HD) * recip[n]).astype(jnp.bfloat16)
        for g in range(GROUP):
            out[
                pl.ds(pl.multiple_of(m * TOK, TOK), TOK),
                pl.ds(pl.multiple_of((head * GROUP + g) * HD, HD), HD),
            ] = mixed[g]
        return 0

    def onward(r):
        @pl.when(even)
        def _():
            x_arrived(other, r)
            x_onward(r).start()

    def ready(b, r):
        if b is other:
            @pl.when(jnp.logical_not(even))
            def _():
                x_arrived(other, r)
        else:
            x_arrived(y, r)

    for t in range(LAG + half + 1):
        if t <= half:
            ring_step(0, t)
        if 0 <= t - LAG <= half:
            ring_step(1, t - LAG)
        if t == 0:
            for r in range(PARTS):
                x_cross(r).start()

                @pl.when(even)
                def _():
                    x_direct(r).start()

            for fetch in fetches[:3]:
                fetch.wait()
            tables()
        if t == 1:
            masks()
            lbuf[...] = jnp.zeros_like(lbuf)
        for r in range(PARTS):
            if t == ONWARD[r]:
                onward(r)
        if t == NORMED - 1:
            for r in range(PARTS):
                ready(other, r)
                normalise(other, r)
        if t == NORMED:
            for r in range(PARTS):
                ready(y, r)
                normalise(y, r)
        for p in range(2):
            k = t - p * LAG
            if t == NORMED:
                for earlier in range(k):
                    add(p, earlier)
            if t >= NORMED and k <= half:
                add(p, k)
            if k == half:
                (keys, values)[p]()
                window_out(p)

    for sub in range(2):
        window_onward(0, sub)
    fetches[3].wait()
    own_arrived(0)
    lax.fori_loop(0, 2, score, 0)
    for sub in range(2):
        window_onward(1, sub)
    lax.fori_loop(2, 4, score, 0)
    others_arrived(0)
    lax.fori_loop(4, 8, score, 0)
    for m in range(MB):
        lse[m] = lbuf[m].T[:QH, :]
    own_arrived(1)
    lax.fori_loop(0, 4, mix, 0)
    others_arrived(1)
    lax.fori_loop(4, 8, mix, 0)

    for p in range(2):
        w_cross(p, y).wait_send()
        for k in range(half):
            for b in (y, other):
                for u in range(SUBS):
                    for upward in (True, False):
                        if hops(k, u, upward):
                            w_hop(p, k, b, u, upward).wait_send()
        for sub in range(2):
            to_up(p, sub).wait_send()
            to_mate_old(p, y, sub).wait_send()
        to_far(p, y).wait_send()
        to_mate(p, y).wait_send()

        @pl.when(y == 0)
        def _():
            to_mate_last(p, y).wait_send()

    for r in range(PARTS):
        x_cross(r).wait_send()

        @pl.when(even)
        def _():
            x_direct(r).wait_send()
            x_onward(r).wait_send()


def solution(mesh):
    sections, n_ctx = mesh.shape["section"], mesh.shape["ctx"]
    ring = n_ctx // 2
    half = ring // 2

    def on_device(handoff, norm_gain, kv_weight, queries, span_order):
        freq = rope_base ** (-2.0 * np.arange(HD // 2, dtype=np.float64) / HD)
        freq = jnp.asarray(np.concatenate([freq, freq])[None].astype(np.float32))
        any_space = pl.BlockSpec(memory_space=pl.ANY)
        vmem = pl.BlockSpec(memory_space=pltpu.VMEM)
        dma = pltpu.SemaphoreType.DMA
        bf16, f32 = jnp.bfloat16, jnp.float32
        out, lse = pl.pallas_call(
            functools.partial(kernel, sections, ring),
            out_shape=(
                pltpu.VMEM((ROWS, D), bf16),
                pltpu.VMEM((MB, QH, TOK), f32),
            ),
            in_specs=[any_space] * 6,
            out_specs=(vmem, vmem),
            scratch_shapes=[
                pltpu.SMEM((MB, n_ctx * 2), jnp.int32),
                pltpu.VMEM((1, HD), f32),
                pltpu.VMEM((1, D), bf16),
                pltpu.VMEM((2, ROWS, D), bf16),
                pltpu.VMEM((2 * ROWS, D), bf16),
                pltpu.VMEM((2, ring, 256, 256), bf16),
                pltpu.VMEM((2, 2 * ROWS, 256), f32),
                pltpu.VMEM((2, KVH, MB, WIN, HD), bf16),
                pltpu.VMEM((ROWS, D), bf16),
                pltpu.VMEM((MB * KVH, GROUP * TOK, SEEN), bf16),
                pltpu.VMEM((MB * KVH, GROUP, TOK, HD), f32),
                pltpu.VMEM((2 * ROWS, HD), f32),
                pltpu.VMEM((2 * ROWS, HD), f32),
                pltpu.VMEM((MB, TOK, SEEN), f32),
                pltpu.VMEM((MB, TOK, HD), f32),
                dma((6,)),
                dma((2, ring, 2, SUBS)),
                dma((2, half, 2, SUBS)),
                dma((2, half, 2, SUBS)),
                dma((2,)),
                dma((2, PARTS)),
                dma((3, PARTS)),
                dma((2, 8)),
                dma((2, 7)),
            ],
            compiler_params=pltpu.CompilerParams(
                collective_id=0, has_side_effects=True, vmem_limit_bytes=56 << 20
            ),
            name="relay",
        )(
            span_order, freq, norm_gain, handoff.reshape(ROWS, D), kv_weight[0], queries.reshape(ROWS, D),
        )
        return out.reshape(1, MB, TOK, D), lse[None]

    placed = (
        P("section", None, "ctx", None),
        P("section", None),
        P("section", "ctx", None),
        P("section", None, "ctx", None),
        P(),
    )
    return jax.shard_map(
        on_device,
        mesh=mesh,
        in_specs=placed,
        out_specs=(P("section", None, "ctx", None), P("section", None, None, "ctx")),
        check_vma=False,
    )
```

```python
import functools
import math

import jax
import jax.numpy as jnp
import numpy as np
from jax import lax
from jax.experimental import pallas as pl
from jax.experimental.pallas import tpu as pltpu
from jax.sharding import PartitionSpec as P

QH = 32
KVH = 4
HD = 128
GROUP = QH // KVH
SPAN = 48
TOK = 96
MB = 2
D = 4096
ROWS = MB * TOK
WIN = 5 * TOK
SEEN = 4 * TOK
MESH = pl.DeviceIdType.MESH
PARTS = 4
PART = ROWS // PARTS
LAG = 0
SUBS = 1
XSTART = (0, 0, 1, 2)
ONWARD = (1, 2, 3, 4)
NORMED = 7
LOG2E = math.log2(math.e)
LN2 = math.log(2.0)
rope_base = 500000.0


def kernel(
    sections, ring,
    order_in, freq_in, gain_in, hand, weight, queries,
    out, lse,
    order, freq, gain, x_buf, xn, w_buf, acc, win, q_buf, probs, recip, cosine, sine, bias, lbuf,
    loc_sem, w_recv, w_up, w_dn, w_mate, x_recv, x_send, win_recv, win_send,
):
    s = lax.axis_index("section")
    c = lax.axis_index("ctx")
    z = c // 2
    y = lax.rem(c, 2)
    other = 1 - y
    mate = 2 * z + other
    half = ring // 2
    even = lax.rem(s, 2) == 0
    nxt = lax.rem(s + 1, sections)
    prv = lax.rem(s + sections - 1, sections)

    def at_z(step):
        return lax.rem(z + step + ring, ring)

    up = {"ctx": 2 * at_z(1) + y}
    dn = {"ctx": 2 * at_z(-1) + y}
    above = {"ctx": 2 * at_z(1)}
    mate_id = {"ctx": mate}

    barrier = pltpu.get_barrier_semaphore()

    def greet(device):
        pl.semaphore_signal(barrier, inc=1, device_id=device, device_id_type=MESH)

    for device in (
        up, dn, mate_id,
        {"section": nxt, "ctx": c}, {"section": prv, "ctx": c},
        {"section": nxt, "ctx": mate}, {"section": prv, "ctx": mate},
    ):
        greet(device)

    @pl.when(y == 0)
    def _():
        greet({"ctx": 2 * at_z(-1) + 1})

    def remote(src, dst, send, recv, device):
        return pltpu.make_async_remote_copy(
            src_ref=src, dst_ref=dst, send_sem=send, recv_sem=recv,
            device_id=device, device_id_type=MESH,
        )

    def w_cols(p, h):
        return weight.at[:, :, pl.ds(pl.multiple_of(p * 512 + h * 256, 256), 256)]

    def w_slot(p, chunk, b):
        return w_buf.at[p, chunk, b]

    def w_local(p):
        return pltpu.make_async_copy(w_cols(p, y), w_slot(p, z, y), loc_sem.at[p])

    def w_cross(p, b):
        return remote(w_cols(p, other), w_slot(p, z, b), w_mate.at[p], w_recv.at[p, z, b, 0], mate_id)

    fetches = [
        pltpu.make_async_copy(src, dst, loc_sem.at[2 + i])
        for i, (src, dst) in enumerate(
            ((order_in, order), (freq_in, freq), (gain_in, gain), (queries, q_buf))
        )
    ]
    for p in range(2):
        w_local(p).start()
    for fetch in fetches:
        fetch.start()

    @pl.when(y == 0)
    def _():
        pl.semaphore_wait(barrier, 7)

    @pl.when(y == 1)
    def _():
        pl.semaphore_wait(barrier, 8)

    for p in range(2):
        w_cross(p, y).start()

    def x_rows(b, r):
        return x_buf.at[b, pl.ds(r * PART, PART)]

    def x_copy(kind, src, b, r, device):
        return remote(src, x_rows(b, r), x_send.at[kind, r], x_recv.at[b, r], device)

    def x_cross(r):
        return x_copy(0, hand.at[pl.ds(r * PART, PART)], y, r, {"section": nxt, "ctx": mate})

    def x_direct(r):
        return x_copy(1, hand.at[pl.ds(r * PART, PART)], y, r, {"section": nxt, "ctx": c})

    def x_onward(r):
        return x_copy(2, x_rows(other, r), other, r, mate_id)

    def x_arrived(b, r):
        x_copy(0, x_rows(b, r), b, r, mate_id).wait_recv()

    def w_hop(p, k, b, u, upward):
        chunk = at_z(-k if upward else k)
        sems = w_up if upward else w_dn
        slot = w_buf.at[p, chunk, b, u]
        src = slot
        if k == 0 and b is y:
            src = w_cols(p, y).at[u]
        return remote(
            src, slot, sems.at[p, k, b, u], w_recv.at[p, chunk, b, u], up if upward else dn
        )

    def hops(k, u, upward):
        if k < half - 1:
            return True
        return k == half - 1 and (u < SUBS // 2) == upward

    def ring_step(p, k):
        for b in (y, other):
            if k == 0 and b is other:
                w_cross(p, other).wait_recv()
            for u in range(SUBS):
                for upward in (True, False):
                    if k > 0 and hops(k - 1, u, upward):
                        w_hop(p, k, b, u, upward).wait_recv()
                    if hops(k, u, upward):
                        w_hop(p, k, b, u, upward).start()

    def slots(p, heads, first, count):
        return win.at[p, heads, :, pl.ds(first * TOK, count * TOK)]

    def pair(h):
        return pl.ds(2 * h, 2)

    def to_up(p, sub):
        head = 2 * y + sub
        return remote(
            slots(p, head, 3, 2), slots(p, head, 1, 2), win_send.at[p, sub], win_recv.at[p, sub], up
        )

    def to_above(p, h):
        return remote(
            slots(p, pair(h), 2, 1), slots(p, pair(h), 0, 1), win_send.at[p, 2], win_recv.at[p, 2 + h], above
        )

    def to_mate(p, h):
        both = slots(p, pair(h), 3, 1)
        return remote(both, both, win_send.at[p, 3], win_recv.at[p, 4], mate_id)

    def to_mate_last(p, h):
        both = slots(p, pair(h), 4, 1)
        return remote(both, both, win_send.at[p, 4], win_recv.at[p, 5], mate_id)

    def to_mate_old(p, h, sub):
        old = slots(p, 2 * h + sub, 1, 2)
        return remote(old, old, win_send.at[p, 5 + sub], win_recv.at[p, 6 + sub], mate_id)

    def window_out(p):
        for sub in range(2):
            to_up(p, sub).start()
        to_mate(p, y).start()

        @pl.when(y == 0)
        def _():
            to_mate_last(p, y).start()

    def window_onward(p, sub):
        to_up(p, sub).wait_recv()
        to_mate_old(p, y, sub).start()
        if sub == 1:
            to_above(p, y).start()

    def own_arrived(p):
        @pl.when(y == 0)
        def _():
            to_above(p, 0).wait_recv()

    def others_arrived(p):
        to_mate(p, other).wait_recv()
        for sub in range(2):
            to_mate_old(p, other, sub).wait_recv()

        @pl.when(y == 0)
        def _():
            to_above(p, 1).wait_recv()

        @pl.when(y == 1)
        def _():
            to_mate_last(p, other).wait_recv()

    def tables():
        row = lax.broadcasted_iota(jnp.int32, (SPAN, HD), 0)
        low = lax.broadcasted_iota(jnp.int32, (SPAN, HD), 1) < HD // 2
        for b in range(2):
            for m in range(MB):
                for i in range(2):
                    span = order[m, 4 * z + 2 * b + i]
                    angle = (span * SPAN + row).astype(jnp.float32) * freq[...]
                    first = b * ROWS + m * TOK + i * SPAN
                    cosine[pl.ds(first, SPAN), :] = jnp.cos(angle)
                    turned = jnp.sin(angle)
                    sine[pl.ds(first, SPAN), :] = jnp.where(low, -turned, turned)

    def masks():
        lane = lax.broadcasted_iota(jnp.int32, (SPAN, SEEN), 1)
        row = lax.broadcasted_iota(jnp.int32, (SPAN, SEEN), 0)
        for m in range(MB):
            key_pos = lane
            for j in range(4):
                block = lax.rem(c - 3 + j + 2 * ring, 2 * ring)
                for i in range(2):
                    n = 2 * j + i
                    here = lane >= n * SPAN
                    key_pos = jnp.where(here, order[m, 2 * block + i] * SPAN + lane - n * SPAN, key_pos)
            for i in range(2):
                own_pos = order[m, 2 * c + i] * SPAN + row
                bias[m, pl.ds(i * SPAN, SPAN), :] = jnp.where(key_pos <= own_pos, 0.0, -jnp.inf)

    def normalise(b, r):
        first = pl.multiple_of(b * ROWS + r * PART, 16)
        values = x_buf[b, pl.ds(r * PART, PART), :].astype(jnp.float32)
        scale = lax.rsqrt(jnp.mean(values * values, axis=-1, keepdims=True) + 1e-05)
        scaled = values * scale * gain[...].astype(jnp.float32)
        xn[pl.ds(first, PART), :] = scaled.astype(jnp.bfloat16)

    def product(p, chunk):
        columns = pl.ds(pl.multiple_of(chunk * 256, 256), 256)
        return jnp.dot(xn[:, columns], w_buf[p, chunk].reshape(256, 256), preferred_element_type=jnp.float32)

    def keys():
        for sub in range(2):
            part = acc[0, :, sub * HD : (sub + 1) * HD]
            turned = part * cosine[...] + pltpu.roll(part, HD // 2, 1) * sine[...]
            store(0, sub, turned)

    def values():
        for sub in range(2):
            store(1, sub, acc[1, :, sub * HD : (sub + 1) * HD])

    def store(p, sub, rows):
        rows = rows.astype(jnp.bfloat16)
        for b in range(2):
            for m in range(MB):
                win[p, 2 * y + sub, m, pl.ds((3 + b) * TOK, TOK), :] = rows[
                    b * ROWS + m * TOK : b * ROWS + (m + 1) * TOK
                ]

    def add(p, k):
        if k == 0:
            w_local(p).wait()
        total = product(p, at_z(k))
        if 0 < k < half:
            total += product(p, at_z(-k))
        if k == 0:
            acc[p] = total
        else:
            acc[p] += total

    def score(n, _):
        m = lax.rem(n, MB)
        head = lax.rem(2 * y + n // MB, KVH)
        q = jnp.concatenate(
            [
                q_buf[pl.ds(pl.multiple_of(m * TOK, TOK), TOK), pl.ds(pl.multiple_of((head * GROUP + g) * HD, HD), HD)]
                for g in range(GROUP)
            ],
            axis=0,
        )
        k = win[0, head, m, pl.ds(pl.multiple_of(y * TOK, TOK), SEEN), :]
        raw = lax.dot_general(q, k, (((1,), (1,)), ((), ())), preferred_element_type=jnp.float32)
        raw = raw.reshape(GROUP, TOK, SEEN) * (HD ** -0.5 * LOG2E) + bias[m][None]
        top = jnp.max(raw, axis=-1, keepdims=True)
        exps = jnp.exp2(raw - top)
        total = jnp.sum(exps, axis=-1, keepdims=True)
        probs[n] = exps.astype(jnp.bfloat16).reshape(GROUP * TOK, SEEN)
        recip[n] = jnp.broadcast_to(1.0 / total, (GROUP, TOK, HD))
        logs = top * LN2 + jnp.log(total)
        lane = lax.broadcasted_iota(jnp.int32, (TOK, HD), 1)
        kept = lbuf[m]
        for g in range(GROUP):
            kept = jnp.where(lane == head * GROUP + g, logs[g], kept)
        lbuf[m] = kept
        return 0

    def mix(n, _):
        m = lax.rem(n, MB)
        head = lax.rem(2 * y + n // MB, KVH)
        v = win[1, head, m, pl.ds(pl.multiple_of(y * TOK, TOK), SEEN), :]
        mixed = jnp.dot(probs[n], v, preferred_element_type=jnp.float32)
        mixed = (mixed.reshape(GROUP, TOK, HD) * recip[n]).astype(jnp.bfloat16)
        for g in range(GROUP):
            out[
                pl.ds(pl.multiple_of(m * TOK, TOK), TOK),
                pl.ds(pl.multiple_of((head * GROUP + g) * HD, HD), HD),
            ] = mixed[g]
        return 0

    def onward(r):
        @pl.when(even)
        def _():
            x_arrived(other, r)
            x_onward(r).start()

    def ready(b, r):
        if b is other:
            @pl.when(jnp.logical_not(even))
            def _():
                x_arrived(other, r)
        else:
            x_arrived(y, r)

    for t in range(LAG + half + 1):
        if t <= half:
            ring_step(0, t)
        if 0 <= t - LAG <= half:
            ring_step(1, t - LAG)
        if t == 0:
            for fetch in fetches[:3]:
                fetch.wait()
            tables()
        if t == 1:
            masks()
            lbuf[...] = jnp.zeros_like(lbuf)
        for r in range(PARTS):
            if t == XSTART[r]:
                if r > 1:
                    x_cross(r - 2).wait_send()
                x_cross(r).start()

                @pl.when(even)
                def _():
                    x_direct(r).start()

            if t == ONWARD[r]:
                onward(r)
        if t == NORMED - 1:
            for r in range(PARTS):
                ready(other, r)
                normalise(other, r)
        if t == NORMED:
            for r in range(PARTS):
                ready(y, r)
                normalise(y, r)
        for p in range(2):
            k = t - p * LAG
            if t == NORMED:
                for earlier in range(min(k, half + 1)):
                    add(p, earlier)
            if t >= NORMED and 0 <= k <= half:
                add(p, k)
            if t == max(NORMED, half + p * LAG):
                (keys, values)[p]()
                window_out(p)

    for p in range(2):
        for sub in range(2):
            window_onward(p, sub)
    fetches[3].wait()
    own_arrived(0)
    lax.fori_loop(0, 4, score, 0)
    others_arrived(0)
    lax.fori_loop(4, 8, score, 0)
    for m in range(MB):
        lse[m] = lbuf[m].T[:QH, :]
    own_arrived(1)
    lax.fori_loop(0, 4, mix, 0)
    others_arrived(1)
    lax.fori_loop(4, 8, mix, 0)

    for p in range(2):
        w_cross(p, y).wait_send()
        for k in range(half):
            for b in (y, other):
                for u in range(SUBS):
                    for upward in (True, False):
                        if hops(k, u, upward):
                            w_hop(p, k, b, u, upward).wait_send()
        for sub in range(2):
            to_up(p, sub).wait_send()
            to_mate_old(p, y, sub).wait_send()
        to_above(p, y).wait_send()
        to_mate(p, y).wait_send()

        @pl.when(y == 0)
        def _():
            to_mate_last(p, y).wait_send()

    for r in range(PARTS):
        if r >= PARTS - 2:
            x_cross(r).wait_send()

        @pl.when(even)
        def _():
            x_direct(r).wait_send()
            x_onward(r).wait_send()


def solution(mesh):
    sections, n_ctx = mesh.shape["section"], mesh.shape["ctx"]
    ring = n_ctx // 2
    half = ring // 2

    def on_device(handoff, norm_gain, kv_weight, queries, span_order):
        freq = rope_base ** (-2.0 * np.arange(HD // 2, dtype=np.float64) / HD)
        freq = jnp.asarray(np.concatenate([freq, freq])[None].astype(np.float32))
        any_space = pl.BlockSpec(memory_space=pl.ANY)
        vmem = pl.BlockSpec(memory_space=pltpu.VMEM)
        dma = pltpu.SemaphoreType.DMA
        bf16, f32 = jnp.bfloat16, jnp.float32
        out, lse = pl.pallas_call(
            functools.partial(kernel, sections, ring),
            out_shape=(
                pltpu.VMEM((ROWS, D), bf16),
                pltpu.VMEM((MB, QH, TOK), f32),
            ),
            in_specs=[any_space] * 6,
            out_specs=(vmem, vmem),
            scratch_shapes=[
                pltpu.SMEM((MB, n_ctx * 2), jnp.int32),
                pltpu.VMEM((1, HD), f32),
                pltpu.VMEM((1, D), bf16),
                pltpu.VMEM((2, ROWS, D), bf16),
                pltpu.VMEM((2 * ROWS, D), bf16),
                pltpu.VMEM((2, ring, 2, SUBS, 128 // SUBS, 256), bf16),
                pltpu.VMEM((2, 2 * ROWS, 256), f32),
                pltpu.VMEM((2, KVH, MB, WIN, HD), bf16),
                pltpu.VMEM((ROWS, D), bf16),
                pltpu.VMEM((MB * KVH, GROUP * TOK, SEEN), bf16),
                pltpu.VMEM((MB * KVH, GROUP, TOK, HD), f32),
                pltpu.VMEM((2 * ROWS, HD), f32),
                pltpu.VMEM((2 * ROWS, HD), f32),
                pltpu.VMEM((MB, TOK, SEEN), f32),
                pltpu.VMEM((MB, TOK, HD), f32),
                dma((6,)),
                dma((2, ring, 2, SUBS)),
                dma((2, half, 2, SUBS)),
                dma((2, half, 2, SUBS)),
                dma((2,)),
                dma((2, PARTS)),
                dma((3, PARTS)),
                dma((2, 8)),
                dma((2, 7)),
            ],
            compiler_params=pltpu.CompilerParams(
                collective_id=0, has_side_effects=True, vmem_limit_bytes=56 << 20
            ),
            name="relay",
        )(
            span_order, freq, norm_gain, handoff.reshape(ROWS, D), kv_weight[0].reshape(SUBS, 128 // SUBS, 1024), queries.reshape(ROWS, D),
        )
        return out.reshape(1, MB, TOK, D), lse[None]

    placed = (
        P("section", None, "ctx", None),
        P("section", None),
        P("section", "ctx", None),
        P("section", None, "ctx", None),
        P(),
    )
    return jax.shard_map(
        on_device,
        mesh=mesh,
        in_specs=placed,
        out_specs=(P("section", None, "ctx", None), P("section", None, None, "ctx")),
        check_vma=False,
    )
```

```python
import functools
import math

import jax
import jax.numpy as jnp
import numpy as np
from jax import lax
from jax.experimental import pallas as pl
from jax.experimental.pallas import tpu as pltpu
from jax.sharding import PartitionSpec as P

QH = 32
KVH = 4
HD = 128
GROUP = QH // KVH
SPAN = 48
TOK = 96
MB = 2
D = 4096
ROWS = MB * TOK
WIN = 5 * TOK
SEEN = 4 * TOK
MESH = pl.DeviceIdType.MESH
PARTS = 4
PART = ROWS // PARTS
LAG = 0
SUBS = 1
XSTART = (0, 0, 1, 2)
ONWARD = (1, 2, 3, 4)
NORMED = 6
LOG2E = math.log2(math.e)
LN2 = math.log(2.0)
rope_base = 500000.0


def kernel(
    sections, ring,
    order_in, freq_in, gain_in, hand, weight, queries,
    out, lse,
    order, freq, gain, x_buf, xn, w_buf, acc, win, q_buf, probs, recip, cosine, sine, bias, lbuf,
    loc_sem, w_recv, w_up, w_dn, w_mate, x_recv, x_send, win_recv, win_send,
):
    s = lax.axis_index("section")
    c = lax.axis_index("ctx")
    z = c // 2
    y = lax.rem(c, 2)
    other = 1 - y
    mate = 2 * z + other
    half = ring // 2
    even = lax.rem(s, 2) == 0
    nxt = lax.rem(s + 1, sections)
    prv = lax.rem(s + sections - 1, sections)

    def at_z(step):
        return lax.rem(z + step + ring, ring)

    up = {"ctx": 2 * at_z(1) + y}
    dn = {"ctx": 2 * at_z(-1) + y}
    above = {"ctx": 2 * at_z(1)}
    mate_id = {"ctx": mate}

    barrier = pltpu.get_barrier_semaphore()

    def greet(device):
        pl.semaphore_signal(barrier, inc=1, device_id=device, device_id_type=MESH)

    for device in (
        up, dn, mate_id,
        {"section": nxt, "ctx": c}, {"section": prv, "ctx": c},
        {"section": nxt, "ctx": mate}, {"section": prv, "ctx": mate},
    ):
        greet(device)

    @pl.when(y == 0)
    def _():
        greet({"ctx": 2 * at_z(-1) + 1})

    def remote(src, dst, send, recv, device):
        return pltpu.make_async_remote_copy(
            src_ref=src, dst_ref=dst, send_sem=send, recv_sem=recv,
            device_id=device, device_id_type=MESH,
        )

    def w_cols(p, h):
        return weight.at[:, :, pl.ds(pl.multiple_of(p * 512 + h * 256, 256), 256)]

    def w_slot(p, chunk, b):
        return w_buf.at[p, chunk, b]

    def w_local(p):
        return pltpu.make_async_copy(w_cols(p, y), w_slot(p, z, y), loc_sem.at[p])

    def w_cross(p, b):
        return remote(w_cols(p, other), w_slot(p, z, b), w_mate.at[p], w_recv.at[p, z, b, 0], mate_id)

    fetches = [
        pltpu.make_async_copy(src, dst, loc_sem.at[2 + i])
        for i, (src, dst) in enumerate(
            ((order_in, order), (freq_in, freq), (gain_in, gain), (queries, q_buf))
        )
    ]
    for p in range(2):
        w_local(p).start()
    for fetch in fetches:
        fetch.start()

    @pl.when(y == 0)
    def _():
        pl.semaphore_wait(barrier, 7)

    @pl.when(y == 1)
    def _():
        pl.semaphore_wait(barrier, 8)

    for p in range(2):
        w_cross(p, y).start()

    def x_rows(b, r):
        return x_buf.at[b, pl.ds(r * PART, PART)]

    def x_copy(kind, src, b, r, device):
        return remote(src, x_rows(b, r), x_send.at[kind, r], x_recv.at[b, r], device)

    def x_cross(r):
        return x_copy(0, hand.at[pl.ds(r * PART, PART)], y, r, {"section": nxt, "ctx": mate})

    def x_direct(r):
        return x_copy(1, hand.at[pl.ds(r * PART, PART)], y, r, {"section": nxt, "ctx": c})

    def x_onward(r):
        return x_copy(2, x_rows(other, r), other, r, mate_id)

    def x_arrived(b, r):
        x_copy(0, x_rows(b, r), b, r, mate_id).wait_recv()

    def w_hop(p, k, b, u, upward):
        chunk = at_z(-k if upward else k)
        sems = w_up if upward else w_dn
        slot = w_buf.at[p, chunk, b, u]
        src = slot
        if k == 0 and b is y:
            src = w_cols(p, y).at[u]
        return remote(
            src, slot, sems.at[p, k, b, u], w_recv.at[p, chunk, b, u], up if upward else dn
        )

    def hops(k, u, upward):
        if k < half - 1:
            return True
        return k == half - 1 and (u < SUBS // 2) == upward

    def ring_step(k):
        for b in (y, other):
            for p in range(2):
                if k == 0 and b is other:
                    w_cross(p, other).wait_recv()
                for u in range(SUBS):
                    for upward in (True, False):
                        if k > 0 and hops(k - 1, u, upward):
                            w_hop(p, k, b, u, upward).wait_recv()
                        if hops(k, u, upward):
                            w_hop(p, k, b, u, upward).start()

    def slots(p, heads, first, count):
        return win.at[p, heads, :, pl.ds(first * TOK, count * TOK)]

    def pair(h):
        return pl.ds(2 * h, 2)

    def to_up(p, sub):
        head = 2 * y + sub
        return remote(
            slots(p, head, 3, 2), slots(p, head, 1, 2), win_send.at[p, sub], win_recv.at[p, sub], up
        )

    def to_above(p, h):
        return remote(
            slots(p, pair(h), 2, 1), slots(p, pair(h), 0, 1), win_send.at[p, 2], win_recv.at[p, 2 + h], above
        )

    def to_mate(p, h):
        both = slots(p, pair(h), 3, 1)
        return remote(both, both, win_send.at[p, 3], win_recv.at[p, 4], mate_id)

    def to_mate_last(p, h):
        both = slots(p, pair(h), 4, 1)
        return remote(both, both, win_send.at[p, 4], win_recv.at[p, 5], mate_id)

    def to_mate_old(p, h, sub):
        old = slots(p, 2 * h + sub, 1, 2)
        return remote(old, old, win_send.at[p, 5 + sub], win_recv.at[p, 6 + sub], mate_id)

    def window_out(p):
        for sub in range(2):
            to_up(p, sub).start()
        to_mate(p, y).start()

        @pl.when(y == 0)
        def _():
            to_mate_last(p, y).start()

    def window_onward(p, sub):
        to_up(p, sub).wait_recv()
        to_mate_old(p, y, sub).start()
        if sub == 1:
            to_above(p, y).start()

    def own_arrived(p):
        @pl.when(y == 0)
        def _():
            to_above(p, 0).wait_recv()

    def others_arrived(p):
        to_mate(p, other).wait_recv()
        for sub in range(2):
            to_mate_old(p, other, sub).wait_recv()

        @pl.when(y == 0)
        def _():
            to_above(p, 1).wait_recv()

        @pl.when(y == 1)
        def _():
            to_mate_last(p, other).wait_recv()

    def tables():
        row = lax.broadcasted_iota(jnp.int32, (SPAN, HD), 0)
        low = lax.broadcasted_iota(jnp.int32, (SPAN, HD), 1) < HD // 2
        for b in range(2):
            for m in range(MB):
                for i in range(2):
                    span = order[m, 4 * z + 2 * b + i]
                    angle = (span * SPAN + row).astype(jnp.float32) * freq[...]
                    first = b * ROWS + m * TOK + i * SPAN
                    cosine[pl.ds(first, SPAN), :] = jnp.cos(angle)
                    turned = jnp.sin(angle)
                    sine[pl.ds(first, SPAN), :] = jnp.where(low, -turned, turned)

    def masks():
        lane = lax.broadcasted_iota(jnp.int32, (SPAN, SEEN), 1)
        row = lax.broadcasted_iota(jnp.int32, (SPAN, SEEN), 0)
        for m in range(MB):
            key_pos = lane
            for j in range(4):
                block = lax.rem(c - 3 + j + 2 * ring, 2 * ring)
                for i in range(2):
                    n = 2 * j + i
                    here = lane >= n * SPAN
                    key_pos = jnp.where(here, order[m, 2 * block + i] * SPAN + lane - n * SPAN, key_pos)
            for i in range(2):
                own_pos = order[m, 2 * c + i] * SPAN + row
                bias[m, pl.ds(i * SPAN, SPAN), :] = jnp.where(key_pos <= own_pos, 0.0, -jnp.inf)

    def normalise(b, r):
        first = pl.multiple_of(b * ROWS + r * PART, 16)
        values = x_buf[b, pl.ds(r * PART, PART), :].astype(jnp.float32)
        scale = lax.rsqrt(jnp.mean(values * values, axis=-1, keepdims=True) + 1e-05)
        scaled = values * scale * gain[...].astype(jnp.float32)
        xn[pl.ds(first, PART), :] = scaled.astype(jnp.bfloat16)

    def product(p, chunk):
        columns = pl.ds(pl.multiple_of(chunk * 256, 256), 256)
        return jnp.dot(xn[:, columns], w_buf[p, chunk].reshape(256, 256), preferred_element_type=jnp.float32)

    def keys():
        for sub in range(2):
            part = acc[0, :, sub * HD : (sub + 1) * HD]
            turned = part * cosine[...] + pltpu.roll(part, HD // 2, 1) * sine[...]
            store(0, sub, turned)

    def values():
        for sub in range(2):
            store(1, sub, acc[1, :, sub * HD : (sub + 1) * HD])

    def store(p, sub, rows):
        rows = rows.astype(jnp.bfloat16)
        for b in range(2):
            for m in range(MB):
                win[p, 2 * y + sub, m, pl.ds((3 + b) * TOK, TOK), :] = rows[
                    b * ROWS + m * TOK : b * ROWS + (m + 1) * TOK
                ]

    def add(p, k):
        if k == 0:
            w_local(p).wait()
        total = product(p, at_z(k))
        if 0 < k < half:
            total += product(p, at_z(-k))
        if k == 0:
            acc[p] = total
        else:
            acc[p] += total

    def score(n, _):
        m = lax.rem(n, MB)
        head = lax.rem(2 * y + n // MB, KVH)
        q = jnp.concatenate(
            [
                q_buf[pl.ds(pl.multiple_of(m * TOK, TOK), TOK), pl.ds(pl.multiple_of((head * GROUP + g) * HD, HD), HD)]
                for g in range(GROUP)
            ],
            axis=0,
        )
        k = win[0, head, m, pl.ds(pl.multiple_of(y * TOK, TOK), SEEN), :]
        raw = lax.dot_general(q, k, (((1,), (1,)), ((), ())), preferred_element_type=jnp.float32)
        raw = raw.reshape(GROUP, TOK, SEEN) * (HD ** -0.5 * LOG2E) + bias[m][None]
        top = jnp.max(raw, axis=-1, keepdims=True)
        exps = jnp.exp2(raw - top)
        total = jnp.sum(exps, axis=-1, keepdims=True)
        probs[n] = exps.astype(jnp.bfloat16).reshape(GROUP * TOK, SEEN)
        recip[n] = jnp.broadcast_to(1.0 / total, (GROUP, TOK, HD))
        logs = top * LN2 + jnp.log(total)
        lane = lax.broadcasted_iota(jnp.int32, (TOK, HD), 1)
        kept = lbuf[m]
        for g in range(GROUP):
            kept = jnp.where(lane == head * GROUP + g, logs[g], kept)
        lbuf[m] = kept
        return 0

    def mix(n, _):
        m = lax.rem(n, MB)
        head = lax.rem(2 * y + n // MB, KVH)
        v = win[1, head, m, pl.ds(pl.multiple_of(y * TOK, TOK), SEEN), :]
        mixed = jnp.dot(probs[n], v, preferred_element_type=jnp.float32)
        mixed = (mixed.reshape(GROUP, TOK, HD) * recip[n]).astype(jnp.bfloat16)
        for g in range(GROUP):
            out[
                pl.ds(pl.multiple_of(m * TOK, TOK), TOK),
                pl.ds(pl.multiple_of((head * GROUP + g) * HD, HD), HD),
            ] = mixed[g]
        return 0

    def onward(r):
        @pl.when(even)
        def _():
            x_arrived(other, r)
            x_onward(r).start()

    def ready(b, r):
        if b is other:
            @pl.when(jnp.logical_not(even))
            def _():
                x_arrived(other, r)
        else:
            x_arrived(y, r)

    for t in range(LAG + half + 1):
        ring_step(t)
        if t == 0:
            for fetch in fetches[:3]:
                fetch.wait()
            tables()
        if t == 1:
            masks()
            lbuf[...] = jnp.zeros_like(lbuf)
        for r in range(PARTS):
            if t == XSTART[r]:
                if r > 1:
                    x_cross(r - 2).wait_send()
                x_cross(r).start()

                @pl.when(even)
                def _():
                    x_direct(r).start()

            if t == ONWARD[r]:
                onward(r)
        if t == NORMED - 1:
            for r in range(PARTS):
                ready(other, r)
                normalise(other, r)
        if t == NORMED:
            for r in range(PARTS):
                ready(y, r)
                normalise(y, r)
        for p in range(2):
            k = t - p * LAG
            if t == NORMED:
                for earlier in range(min(k, half + 1)):
                    add(p, earlier)
            if t >= NORMED and 0 <= k <= half:
                add(p, k)
            if t == max(NORMED, half + p * LAG):
                (keys, values)[p]()
                window_out(p)

    for p in range(2):
        for sub in range(2):
            window_onward(p, sub)
    fetches[3].wait()
    own_arrived(0)
    lax.fori_loop(0, 4, score, 0)
    others_arrived(0)
    lax.fori_loop(4, 8, score, 0)
    for m in range(MB):
        lse[m] = lbuf[m].T[:QH, :]
    own_arrived(1)
    lax.fori_loop(0, 4, mix, 0)
    others_arrived(1)
    lax.fori_loop(4, 8, mix, 0)

    for p in range(2):
        w_cross(p, y).wait_send()
        for k in range(half):
            for b in (y, other):
                for u in range(SUBS):
                    for upward in (True, False):
                        if hops(k, u, upward):
                            w_hop(p, k, b, u, upward).wait_send()
        for sub in range(2):
            to_up(p, sub).wait_send()
            to_mate_old(p, y, sub).wait_send()
        to_above(p, y).wait_send()
        to_mate(p, y).wait_send()

        @pl.when(y == 0)
        def _():
            to_mate_last(p, y).wait_send()

    for r in range(PARTS):
        if r >= PARTS - 2:
            x_cross(r).wait_send()

        @pl.when(even)
        def _():
            x_direct(r).wait_send()
            x_onward(r).wait_send()


def solution(mesh):
    sections, n_ctx = mesh.shape["section"], mesh.shape["ctx"]
    ring = n_ctx // 2
    half = ring // 2

    def on_device(handoff, norm_gain, kv_weight, queries, span_order):
        freq = rope_base ** (-2.0 * np.arange(HD // 2, dtype=np.float64) / HD)
        freq = jnp.asarray(np.concatenate([freq, freq])[None].astype(np.float32))
        any_space = pl.BlockSpec(memory_space=pl.ANY)
        vmem = pl.BlockSpec(memory_space=pltpu.VMEM)
        dma = pltpu.SemaphoreType.DMA
        bf16, f32 = jnp.bfloat16, jnp.float32
        out, lse = pl.pallas_call(
            functools.partial(kernel, sections, ring),
            out_shape=(
                pltpu.VMEM((ROWS, D), bf16),
                pltpu.VMEM((MB, QH, TOK), f32),
            ),
            in_specs=[any_space] * 6,
            out_specs=(vmem, vmem),
            scratch_shapes=[
                pltpu.SMEM((MB, n_ctx * 2), jnp.int32),
                pltpu.VMEM((1, HD), f32),
                pltpu.VMEM((1, D), bf16),
                pltpu.VMEM((2, ROWS, D), bf16),
                pltpu.VMEM((2 * ROWS, D), bf16),
                pltpu.VMEM((2, ring, 2, SUBS, 128 // SUBS, 256), bf16),
                pltpu.VMEM((2, 2 * ROWS, 256), f32),
                pltpu.VMEM((2, KVH, MB, WIN, HD), bf16),
                pltpu.VMEM((ROWS, D), bf16),
                pltpu.VMEM((MB * KVH, GROUP * TOK, SEEN), bf16),
                pltpu.VMEM((MB * KVH, GROUP, TOK, HD), f32),
                pltpu.VMEM((2 * ROWS, HD), f32),
                pltpu.VMEM((2 * ROWS, HD), f32),
                pltpu.VMEM((MB, TOK, SEEN), f32),
                pltpu.VMEM((MB, TOK, HD), f32),
                dma((6,)),
                dma((2, ring, 2, SUBS)),
                dma((2, half, 2, SUBS)),
                dma((2, half, 2, SUBS)),
                dma((2,)),
                dma((2, PARTS)),
                dma((3, PARTS)),
                dma((2, 8)),
                dma((2, 7)),
            ],
            compiler_params=pltpu.CompilerParams(
                collective_id=0, has_side_effects=True, vmem_limit_bytes=56 << 20
            ),
            name="relay",
        )(
            span_order, freq, norm_gain, handoff.reshape(ROWS, D), kv_weight[0].reshape(SUBS, 128 // SUBS, 1024), queries.reshape(ROWS, D),
        )
        return out.reshape(1, MB, TOK, D), lse[None]

    placed = (
        P("section", None, "ctx", None),
        P("section", None),
        P("section", "ctx", None),
        P("section", None, "ctx", None),
        P(),
    )
    return jax.shard_map(
        on_device,
        mesh=mesh,
        in_specs=placed,
        out_specs=(P("section", None, "ctx", None), P("section", None, None, "ctx")),
        check_vma=False,
    )
```

```python
import functools
import math

import jax
import jax.numpy as jnp
import numpy as np
from jax import lax
from jax.experimental import pallas as pl
from jax.experimental.pallas import tpu as pltpu
from jax.sharding import PartitionSpec as P

QH = 32
KVH = 4
HD = 128
GROUP = QH // KVH
SPAN = 48
TOK = 96
MB = 2
D = 4096
ROWS = MB * TOK
WIN = 5 * TOK
SEEN = 4 * TOK
MESH = pl.DeviceIdType.MESH
PARTS = 4
PART = ROWS // PARTS
LAG = 0
SUBS = 1
XSTART = (0, 0, 1, 2)
ONWARD = (1, 2, 3, 4)
NORMED = 6
LOG2E = math.log2(math.e)
LN2 = math.log(2.0)
rope_base = 500000.0


def kernel(
    sections, ring,
    order_in, freq_in, gain_in, hand, weight, queries,
    out, lse,
    order, freq, gain, x_buf, xn, w_buf, acc, win, q_buf, probs, recip, cosine, sine, bias, lbuf,
    loc_sem, w_recv, w_up, w_dn, w_mate, x_recv, x_send, win_recv, win_send,
):
    s = lax.axis_index("section")
    c = lax.axis_index("ctx")
    z = c // 2
    y = lax.rem(c, 2)
    other = 1 - y
    mate = 2 * z + other
    half = ring // 2
    even = lax.rem(s, 2) == 0
    nxt = lax.rem(s + 1, sections)
    prv = lax.rem(s + sections - 1, sections)

    def at_z(step):
        return lax.rem(z + step + ring, ring)

    up = {"ctx": 2 * at_z(1) + y}
    dn = {"ctx": 2 * at_z(-1) + y}
    above = {"ctx": 2 * at_z(1)}
    mate_id = {"ctx": mate}

    barrier = pltpu.get_barrier_semaphore()

    def greet(device):
        pl.semaphore_signal(barrier, inc=1, device_id=device, device_id_type=MESH)

    for device in (
        up, dn, mate_id,
        {"section": nxt, "ctx": c}, {"section": prv, "ctx": c},
        {"section": nxt, "ctx": mate}, {"section": prv, "ctx": mate},
    ):
        greet(device)

    @pl.when(y == 0)
    def _():
        greet({"ctx": 2 * at_z(-1) + 1})

    def remote(src, dst, send, recv, device):
        return pltpu.make_async_remote_copy(
            src_ref=src, dst_ref=dst, send_sem=send, recv_sem=recv,
            device_id=device, device_id_type=MESH,
        )

    def w_cols(p, h):
        return weight.at[:, :, pl.ds(pl.multiple_of(p * 512 + h * 256, 256), 256)]

    def w_slot(p, chunk, b):
        return w_buf.at[p, chunk, b]

    def w_local(p):
        return pltpu.make_async_copy(w_cols(p, y), w_slot(p, z, y), loc_sem.at[p])

    def w_cross(p, b):
        return remote(w_cols(p, other), w_slot(p, z, b), w_mate.at[p], w_recv.at[p, z, b, 0], mate_id)

    fetches = [
        pltpu.make_async_copy(src, dst, loc_sem.at[2 + i])
        for i, (src, dst) in enumerate(
            ((order_in, order), (freq_in, freq), (gain_in, gain), (queries, q_buf))
        )
    ]
    for p in range(2):
        w_local(p).start()
    for fetch in fetches:
        fetch.start()

    @pl.when(y == 0)
    def _():
        pl.semaphore_wait(barrier, 7)

    @pl.when(y == 1)
    def _():
        pl.semaphore_wait(barrier, 8)

    for p in range(2):
        w_cross(p, y).start()

    def x_rows(b, r):
        return x_buf.at[b, pl.ds(r * PART, PART)]

    def x_copy(kind, src, b, r, device):
        return remote(src, x_rows(b, r), x_send.at[kind, r], x_recv.at[b, r], device)

    def x_cross(r):
        return x_copy(0, hand.at[pl.ds(r * PART, PART)], y, r, {"section": nxt, "ctx": mate})

    def x_direct(r):
        return x_copy(1, hand.at[pl.ds(r * PART, PART)], y, r, {"section": nxt, "ctx": c})

    def x_onward(r):
        return x_copy(2, x_rows(other, r), other, r, mate_id)

    def x_arrived(b, r):
        x_copy(0, x_rows(b, r), b, r, mate_id).wait_recv()

    def w_hop(p, k, b, u, upward):
        chunk = at_z(-k if upward else k)
        sems = w_up if upward else w_dn
        slot = w_buf.at[p, chunk, b, u]
        src = slot
        if k == 0 and b is y:
            src = w_cols(p, y).at[u]
        return remote(
            src, slot, sems.at[p, k, b, u], w_recv.at[p, chunk, b, u], up if upward else dn
        )

    def hops(k, u, upward):
        if k < half - 1:
            return True
        return k == half - 1 and (u < SUBS // 2) == upward

    def ring_step(k):
        for b in (y, other):
            for p in range(2):
                if k == 0 and b is other:
                    w_cross(p, other).wait_recv()
                for u in range(SUBS):
                    for upward in (True, False):
                        if k > 0 and hops(k - 1, u, upward):
                            w_hop(p, k, b, u, upward).wait_recv()
                        if hops(k, u, upward):
                            w_hop(p, k, b, u, upward).start()

    def slots(p, heads, first, count):
        return win.at[p, heads, :, pl.ds(first * TOK, count * TOK)]

    def pair(h):
        return pl.ds(2 * h, 2)

    def to_up(p, sub):
        head = 2 * y + sub
        return remote(
            slots(p, head, 3, 2), slots(p, head, 1, 2), win_send.at[p, sub], win_recv.at[p, sub], up
        )

    def to_above(p, h):
        return remote(
            slots(p, pair(h), 2, 1), slots(p, pair(h), 0, 1), win_send.at[p, 2], win_recv.at[p, 2 + h], above
        )

    def to_mate(p, h):
        both = slots(p, pair(h), 3, 1)
        return remote(both, both, win_send.at[p, 3], win_recv.at[p, 4], mate_id)

    def to_mate_last(p, h):
        both = slots(p, pair(h), 4, 1)
        return remote(both, both, win_send.at[p, 4], win_recv.at[p, 5], mate_id)

    def to_mate_old(p, h, sub):
        old = slots(p, 2 * h + sub, 1, 2)
        return remote(old, old, win_send.at[p, 5 + sub], win_recv.at[p, 6 + sub], mate_id)

    def window_out(p):
        to_mate(p, y).start()

        @pl.when(y == 0)
        def _():
            to_mate_last(p, y).start()

        for sub in range(2):
            to_up(p, sub).start()

    def window_onward(p, sub):
        to_up(p, sub).wait_recv()
        to_mate_old(p, y, sub).start()
        if sub == 1:
            to_above(p, y).start()

    def own_arrived(p):
        @pl.when(y == 0)
        def _():
            to_above(p, 0).wait_recv()

    def others_arrived(p):
        to_mate(p, other).wait_recv()
        for sub in range(2):
            to_mate_old(p, other, sub).wait_recv()

        @pl.when(y == 0)
        def _():
            to_above(p, 1).wait_recv()

        @pl.when(y == 1)
        def _():
            to_mate_last(p, other).wait_recv()

    def tables():
        row = lax.broadcasted_iota(jnp.int32, (SPAN, HD), 0)
        low = lax.broadcasted_iota(jnp.int32, (SPAN, HD), 1) < HD // 2
        for b in range(2):
            for m in range(MB):
                for i in range(2):
                    span = order[m, 4 * z + 2 * b + i]
                    angle = (span * SPAN + row).astype(jnp.float32) * freq[...]
                    first = b * ROWS + m * TOK + i * SPAN
                    cosine[pl.ds(first, SPAN), :] = jnp.cos(angle)
                    turned = jnp.sin(angle)
                    sine[pl.ds(first, SPAN), :] = jnp.where(low, -turned, turned)

    def masks():
        lane = lax.broadcasted_iota(jnp.int32, (SPAN, SEEN), 1)
        row = lax.broadcasted_iota(jnp.int32, (SPAN, SEEN), 0)
        for m in range(MB):
            key_pos = lane
            for j in range(4):
                block = lax.rem(c - 3 + j + 2 * ring, 2 * ring)
                for i in range(2):
                    n = 2 * j + i
                    here = lane >= n * SPAN
                    key_pos = jnp.where(here, order[m, 2 * block + i] * SPAN + lane - n * SPAN, key_pos)
            for i in range(2):
                own_pos = order[m, 2 * c + i] * SPAN + row
                bias[m, pl.ds(i * SPAN, SPAN), :] = jnp.where(key_pos <= own_pos, 0.0, -jnp.inf)

    def normalise(b, r):
        first = pl.multiple_of(b * ROWS + r * PART, 16)
        values = x_buf[b, pl.ds(r * PART, PART), :].astype(jnp.float32)
        scale = lax.rsqrt(jnp.mean(values * values, axis=-1, keepdims=True) + 1e-05)
        scaled = values * scale * gain[...].astype(jnp.float32)
        xn[pl.ds(first, PART), :] = scaled.astype(jnp.bfloat16)

    def product(p, chunk):
        columns = pl.ds(pl.multiple_of(chunk * 256, 256), 256)
        return jnp.dot(xn[:, columns], w_buf[p, chunk].reshape(256, 256), preferred_element_type=jnp.float32)

    def keys():
        for sub in range(2):
            part = acc[0, :, sub * HD : (sub + 1) * HD]
            turned = part * cosine[...] + pltpu.roll(part, HD // 2, 1) * sine[...]
            store(0, sub, turned)

    def values():
        for sub in range(2):
            store(1, sub, acc[1, :, sub * HD : (sub + 1) * HD])

    def store(p, sub, rows):
        rows = rows.astype(jnp.bfloat16)
        for b in range(2):
            for m in range(MB):
                win[p, 2 * y + sub, m, pl.ds((3 + b) * TOK, TOK), :] = rows[
                    b * ROWS + m * TOK : b * ROWS + (m + 1) * TOK
                ]

    def add(p, k):
        if k == 0:
            w_local(p).wait()
        total = product(p, at_z(k))
        if 0 < k < half:
            total += product(p, at_z(-k))
        if k == 0:
            acc[p] = total
        else:
            acc[p] += total

    def score(n, _):
        m = lax.rem(n, MB)
        head = lax.rem(2 * y + n // MB, KVH)
        q = jnp.concatenate(
            [
                q_buf[pl.ds(pl.multiple_of(m * TOK, TOK), TOK), pl.ds(pl.multiple_of((head * GROUP + g) * HD, HD), HD)]
                for g in range(GROUP)
            ],
            axis=0,
        )
        k = win[0, head, m, pl.ds(pl.multiple_of(y * TOK, TOK), SEEN), :]
        raw = lax.dot_general(q, k, (((1,), (1,)), ((), ())), preferred_element_type=jnp.float32)
        raw = raw.reshape(GROUP, TOK, SEEN) * (HD ** -0.5 * LOG2E) + bias[m][None]
        top = jnp.max(raw, axis=-1, keepdims=True)
        exps = jnp.exp2(raw - top)
        total = jnp.sum(exps, axis=-1, keepdims=True)
        probs[n] = exps.astype(jnp.bfloat16).reshape(GROUP * TOK, SEEN)
        recip[n] = jnp.broadcast_to(1.0 / total, (GROUP, TOK, HD))
        logs = top * LN2 + jnp.log(total)
        lane = lax.broadcasted_iota(jnp.int32, (TOK, HD), 1)
        kept = lbuf[m]
        for g in range(GROUP):
            kept = jnp.where(lane == head * GROUP + g, logs[g], kept)
        lbuf[m] = kept
        return 0

    def mix(n, _):
        m = lax.rem(n, MB)
        head = lax.rem(2 * y + n // MB, KVH)
        v = win[1, head, m, pl.ds(pl.multiple_of(y * TOK, TOK), SEEN), :]
        mixed = jnp.dot(probs[n], v, preferred_element_type=jnp.float32)
        mixed = (mixed.reshape(GROUP, TOK, HD) * recip[n]).astype(jnp.bfloat16)
        for g in range(GROUP):
            out[
                pl.ds(pl.multiple_of(m * TOK, TOK), TOK),
                pl.ds(pl.multiple_of((head * GROUP + g) * HD, HD), HD),
            ] = mixed[g]
        return 0

    def onward(r):
        @pl.when(even)
        def _():
            x_arrived(other, r)
            x_onward(r).start()

    def ready(b, r):
        if b is other:
            @pl.when(jnp.logical_not(even))
            def _():
                x_arrived(other, r)
        else:
            x_arrived(y, r)

    for t in range(LAG + half + 1):
        ring_step(t)
        if t == 0:
            for fetch in fetches[:3]:
                fetch.wait()
            tables()
        if t == 1:
            masks()
            lbuf[...] = jnp.zeros_like(lbuf)
        for r in range(PARTS):
            if t == XSTART[r]:
                if r > 1:
                    x_cross(r - 2).wait_send()
                x_cross(r).start()

                @pl.when(even)
                def _():
                    x_direct(r).start()

            if t == ONWARD[r]:
                onward(r)
        if t == NORMED - 1:
            for r in range(PARTS):
                ready(other, r)
                normalise(other, r)
        if t == NORMED:
            for r in range(PARTS):
                ready(y, r)
                normalise(y, r)
        for p in range(2):
            k = t - p * LAG
            if t == NORMED:
                for earlier in range(min(k, half + 1)):
                    add(p, earlier)
            if t >= NORMED and 0 <= k <= half:
                add(p, k)
            if t == max(NORMED, half + p * LAG):
                (keys, values)[p]()
                window_out(p)

    for p in range(2):
        for sub in range(2):
            window_onward(p, sub)
    fetches[3].wait()
    own_arrived(0)
    lax.fori_loop(0, 4, score, 0)
    others_arrived(0)
    lax.fori_loop(4, 8, score, 0)
    for m in range(MB):
        lse[m] = lbuf[m].T[:QH, :]
    own_arrived(1)
    lax.fori_loop(0, 4, mix, 0)
    others_arrived(1)
    lax.fori_loop(4, 8, mix, 0)

    for p in range(2):
        w_cross(p, y).wait_send()
        for k in range(half):
            for b in (y, other):
                for u in range(SUBS):
                    for upward in (True, False):
                        if hops(k, u, upward):
                            w_hop(p, k, b, u, upward).wait_send()
        for sub in range(2):
            to_up(p, sub).wait_send()
            to_mate_old(p, y, sub).wait_send()
        to_above(p, y).wait_send()
        to_mate(p, y).wait_send()

        @pl.when(y == 0)
        def _():
            to_mate_last(p, y).wait_send()

    for r in range(PARTS):
        if r >= PARTS - 2:
            x_cross(r).wait_send()

        @pl.when(even)
        def _():
            x_direct(r).wait_send()
            x_onward(r).wait_send()


def solution(mesh):
    sections, n_ctx = mesh.shape["section"], mesh.shape["ctx"]
    ring = n_ctx // 2
    half = ring // 2

    def on_device(handoff, norm_gain, kv_weight, queries, span_order):
        freq = rope_base ** (-2.0 * np.arange(HD // 2, dtype=np.float64) / HD)
        freq = jnp.asarray(np.concatenate([freq, freq])[None].astype(np.float32))
        any_space = pl.BlockSpec(memory_space=pl.ANY)
        vmem = pl.BlockSpec(memory_space=pltpu.VMEM)
        dma = pltpu.SemaphoreType.DMA
        bf16, f32 = jnp.bfloat16, jnp.float32
        out, lse = pl.pallas_call(
            functools.partial(kernel, sections, ring),
            out_shape=(
                pltpu.VMEM((ROWS, D), bf16),
                pltpu.VMEM((MB, QH, TOK), f32),
            ),
            in_specs=[any_space] * 6,
            out_specs=(vmem, vmem),
            scratch_shapes=[
                pltpu.SMEM((MB, n_ctx * 2), jnp.int32),
                pltpu.VMEM((1, HD), f32),
                pltpu.VMEM((1, D), bf16),
                pltpu.VMEM((2, ROWS, D), bf16),
                pltpu.VMEM((2 * ROWS, D), bf16),
                pltpu.VMEM((2, ring, 2, SUBS, 128 // SUBS, 256), bf16),
                pltpu.VMEM((2, 2 * ROWS, 256), f32),
                pltpu.VMEM((2, KVH, MB, WIN, HD), bf16),
                pltpu.VMEM((ROWS, D), bf16),
                pltpu.VMEM((MB * KVH, GROUP * TOK, SEEN), bf16),
                pltpu.VMEM((MB * KVH, GROUP, TOK, HD), f32),
                pltpu.VMEM((2 * ROWS, HD), f32),
                pltpu.VMEM((2 * ROWS, HD), f32),
                pltpu.VMEM((MB, TOK, SEEN), f32),
                pltpu.VMEM((MB, TOK, HD), f32),
                dma((6,)),
                dma((2, ring, 2, SUBS)),
                dma((2, half, 2, SUBS)),
                dma((2, half, 2, SUBS)),
                dma((2,)),
                dma((2, PARTS)),
                dma((3, PARTS)),
                dma((2, 8)),
                dma((2, 7)),
            ],
            compiler_params=pltpu.CompilerParams(
                collective_id=0, has_side_effects=True, vmem_limit_bytes=56 << 20
            ),
            name="relay",
        )(
            span_order, freq, norm_gain, handoff.reshape(ROWS, D), kv_weight[0].reshape(SUBS, 128 // SUBS, 1024), queries.reshape(ROWS, D),
        )
        return out.reshape(1, MB, TOK, D), lse[None]

    placed = (
        P("section", None, "ctx", None),
        P("section", None),
        P("section", "ctx", None),
        P("section", None, "ctx", None),
        P(),
    )
    return jax.shard_map(
        on_device,
        mesh=mesh,
        in_specs=placed,
        out_specs=(P("section", None, "ctx", None), P("section", None, None, "ctx")),
        check_vma=False,
    )
```
